32 devices in a mesh: dp: 8 (over z, x), tensor: 4 (over y, core).
Axes of the slice: x: 2, y: 2, z: 4, core: 2. Of those that a mesh axis runs over, the one named last changes fastest.
Arguments:
- layer_input: bfloat16 [24576, 768], P(('dp', 'tensor')), may hold values from -6 to 6
- output_grad: bfloat16 [24576, 768], P(('dp', 'tensor')), may hold values from -6 to 6
- source_row: int32 [24576], P(('dp', 'tensor')), may hold values from 0 to 24575, as said below
- dest_row: int32 [24576], P(('dp', 'tensor')), may hold values from 0 to 24575, as said below
- seq_lengths: int32 [24], P('dp'), may hold values from 1 to 1024, 15360 in all
- w_qkv: bfloat16 [768, 3, 768], P('dp', None, 'tensor'), may hold values from -0.3125 to 0.3125
- w_out: bfloat16 [768, 768], P('tensor', 'dp'), may hold values from -1.25 to 1.25
- gain_attn: bfloat16 [768], P('dp'), may hold values from 0.5 to 1.5
- bias_attn: bfloat16 [768], P('dp'), may hold values from -3 to 3
- w_gate_up: bfloat16 [768, 2, 3072], P('dp', None, 'tensor'), may hold values from -0.21875 to 0.21875
- w_down: bfloat16 [3072, 768], P('tensor', 'dp'), may hold values from -0.21875 to 0.21875
- gain_ffn: bfloat16 [768], P('dp'), may hold values from 0.5 to 1.5
- bias_ffn: bfloat16 [768], P('dp'), may hold values from -3 to 3
Outputs:
- layer_output: bfloat16 [24576, 768], P(('dp', 'tensor'))
- input_grad: bfloat16 [24576, 768], P(('dp', 'tensor'))
- qkv_grad: float32 [768, 3, 768], P('dp', None, 'tensor')
- out_grad: float32 [768, 768], P('tensor', 'dp')
- gain_attn_grad: float32 [768], P('dp')
- bias_attn_grad: float32 [768], P('dp')
- gate_up_grad: float32 [768, 2, 3072], P('dp', None, 'tensor')
- down_grad: float32 [3072, 768], P('tensor', 'dp')
- gain_ffn_grad: float32 [768], P('dp')
- bias_ffn_grad: float32 [768], P('dp')
- clipped_qkv: float32 [768, 3, 768], P('dp', None, 'tensor')
The draws below stay inside these ranges and needn't reach their ends.
Inputs may be any that keep to these rules, and one draw needn't show every extreme that they name: A permutation: working row w takes input row source_row[w]. Rows are numbered by dp index, then tensor index, then the 768 rows of a device. A working row and its input row have the same tensor index, and the 768 working rows of any device take exactly 96 input rows from each dp index. The inverse permutation: dest_row[source_row[w]] = w. Working rows k * 1024 to (k + 1) * 1024 - 1 hold sequence k; its first seq_lengths[k] rows are tokens, the rest padding. The lengths sum to 15360.
All inputs are finite; a program needn't handle non-finite values. No bound on the sum of `seq_lengths` on one device may be relied on, other than what follows from the above.
Results may differ from the reference program's by a relative error of at most 0.024.
Values may be sent and summed in bfloat16 or wider, within the bound.
No kernel may reach another device: no remote copies, remote signals or barrier semaphores. Data moves between devices by JAX's collectives and lax.ppermute only.
A program may use at most 192 MiB of HBM per device.

```python
import math
import jax
import jax.numpy as jnp
import numpy as np
from jax import lax

D = 768
H = 12
HD = 64
FF = 3072
ROPE_BASE = 1000
MAXLEN = 1024
CLIP_AT = 4
SEQ_GRP = 3
TOK_DEV = 768
NSEQ = 24
TOKENS = 24576
LIVE = 15360
N_DP = 8
N_TENSOR = 4


def random_orders(seed_key, leading, count):
    scores = jax.random.randint(seed_key, leading + (count,), 0, 4096) * count + jnp.arange(count)
    return jnp.argsort(scores, axis=-1).astype(jnp.int32)


def deal_tables(key):
    dp_count = NSEQ // SEQ_GRP
    row_count = TOK_DEV
    tensor_count = SEQ_GRP * MAXLEN // TOK_DEV
    pair_rows = row_count // dp_count
    key_peer, key_pick, key_spot = jax.random.split(jax.random.fold_in(key, 11), 3)
    peers = random_orders(key_peer, (tensor_count, dp_count), dp_count)
    picks = random_orders(key_pick, (tensor_count, dp_count), row_count)
    spots = random_orders(key_spot, (tensor_count, dp_count), row_count)
    slot_index = jnp.arange(row_count)
    sender = peers[:, :, slot_index // pair_rows]
    tensor_index = jnp.arange(tensor_count)[:, None, None]
    group_index = jnp.arange(dp_count)[None, :, None]
    within = picks[tensor_index, sender, group_index * pair_rows + (slot_index % pair_rows)[None, None, :]]
    anchor = (sender * tensor_count + tensor_index) * row_count + within
    placed = jnp.zeros((tensor_count, dp_count, row_count), jnp.int32).at[tensor_index, group_index, spots].set(anchor.astype(jnp.int32))
    source_table = jnp.transpose(placed, (1, 0, 2)).reshape(-1)
    total_rows = dp_count * tensor_count * row_count
    dest_table = jnp.zeros((total_rows,), jnp.int32).at[source_table].set(jnp.arange(total_rows, dtype=jnp.int32))
    return (source_table, dest_table)


def draw_source_row(key, part):
    return deal_tables(key)[0]


def draw_dest_row(key, part):
    return deal_tables(key)[1]


def level_of(stream_key, dims, shards, least, top_value):
    loudness, own = 1.0, jax.random.fold_in(stream_key, 6)
    for axis_at, shards_of in shards:
        draws = jnp.exp(jax.random.uniform(jax.random.fold_in(own, axis_at), (shards_of,), jnp.float32, least / len(shards), top_value / len(shards)))
        loudness = loudness * jnp.repeat(draws, dims[axis_at] // shards_of).reshape([-1 if axis == axis_at else 1 for axis in range(len(dims))])
    return loudness


def length_profile(number_of, total, limit, slope):
    weights = [(1 << 20) // math.isqrt(grade ** slope) + 1 for grade in range(2, number_of + 1)]
    rest, counts = total - limit - (number_of - 1), [1] * (number_of - 1)
    while rest > 0:
        free = [i for i in range(number_of - 1) if counts[i] < limit]
        pool, remaining = sum([weights[i] for i in free]), rest
        for i in free:
            addition = min(limit - counts[i], max(1, remaining * weights[i] // pool), rest)
            counts[i] = counts[i] + addition
            rest = rest - addition
    return np.array([limit] + counts)


def uneven(rng, count, total, limit, slope):
    if count == 2:
        one = jax.random.randint(rng, (), max(1, total - limit), min(limit, total - 1) + 1)
        return jnp.stack([one, total - one])
    sizes = jnp.asarray(length_profile(count, total, limit, slope), jnp.int32)
    couples = (count - 1) // 2
    giver, taker = sizes[1:1 + 2 * couples:2], sizes[2:2 + 2 * couples:2]
    slack = jnp.minimum(giver - 1, limit - taker)
    passed = jax.random.randint(jax.random.fold_in(rng, 1), (couples,), 0, 1 << 20) % (slack + 1)
    sizes = sizes.at[1:1 + 2 * couples:2].set(giver - passed).at[2:2 + 2 * couples:2].set(taker + passed)
    return sizes[jax.random.permutation(jax.random.fold_in(rng, 2), count)]


def noise(key, shape, scale, limit, cuts=(), kind=jnp.bfloat16):
    drawn = scale * jax.random.normal(key, shape, jnp.float32)
    if cuts:
        drawn = drawn * level_of(key, shape, cuts, -0.22, 0.18)
    return jnp.clip(drawn, -limit, limit).astype(kind)


def setup_inputs(seed: int = 0) -> dict:
    streams_of = jax.random.split(jax.random.key(seed), 14)
    layer_input = noise(streams_of[0], (TOKENS, D), 1.0, 6.0, ((0, 32),))
    output_grad = noise(streams_of[1], (TOKENS, D), 1.0, 6.0, ((0, 32),))
    source_row = draw_source_row(jax.random.fold_in(streams_of[13], 71), 0)
    dest_row = draw_dest_row(jax.random.fold_in(streams_of[13], 71), 0)
    seq_lengths = uneven(streams_of[4], NSEQ, LIVE, MAXLEN, 2).astype(jnp.int32)
    w_qkv = noise(streams_of[5], (D, 3, D), (D // 2) ** -0.5, 0.3125, ((0, 8), (2, 4)))
    w_out = noise(streams_of[6], (D, D), (D // 32) ** -0.5, 1.25, ((0, 4), (1, 8)))
    gain_attn = jnp.clip(1.0 + 0.1 * jax.random.normal(streams_of[7], (D,), jnp.float32), 0.5, 1.5).astype(jnp.bfloat16)
    bias_attn = noise(streams_of[8], (D,), 0.5, 3.0, ((0, 8),))
    w_gate_up = noise(streams_of[9], (D, 2, FF), D ** -0.5, 0.21875, ((0, 8), (2, 4)))
    w_down = noise(streams_of[10], (FF, D), (FF // 4) ** -0.5, 0.21875, ((0, 4), (1, 8)))
    gain_ffn = jnp.clip(1.0 + 0.1 * jax.random.normal(streams_of[11], (D,), jnp.float32), 0.5, 1.5).astype(jnp.bfloat16)
    bias_ffn = noise(streams_of[12], (D,), 0.5, 3.0, ((0, 8),))
    return {"layer_input": layer_input, "output_grad": output_grad, "source_row": source_row, "dest_row": dest_row, "seq_lengths": seq_lengths, "w_qkv": w_qkv, "w_out": w_out, "gain_attn": gain_attn, "bias_attn": bias_attn, "w_gate_up": w_gate_up, "w_down": w_down, "gain_ffn": gain_ffn, "bias_ffn": bias_ffn}


HIGH = lax.Precision.HIGHEST
NEG_FILL = -1e+30
NORM_EPS = 1e-12

@jax.custom_vjp
def low(v):
    return lax.optimization_barrier(v.astype(jnp.bfloat16)).astype(jnp.float32)

@jax.custom_vjp
def low_back(v):
    return v

def low_keep(v):
    return (low(v), None)

def low_pass(kept, grad):
    return (grad,)

def back_keep(v):
    return (v, None)

def back_low(kept, grad):
    return (low(grad),)
low.defvjp(low_keep, low_pass)
low_back.defvjp(back_keep, back_low)

def matmul(left, right):
    return jnp.tensordot(left, right, axes=1, precision=HIGH)

def layer_norm(values, gain_vec, shift_vec):
    centred = values - lax.optimization_barrier(jnp.mean(values, axis=-1, keepdims=True))
    inverse = lax.rsqrt(lax.optimization_barrier(jnp.mean(centred * centred, axis=-1, keepdims=True)) + NORM_EPS)
    return centred * inverse * gain_vec + shift_vec

def rotary_tables(count):
    half_dim = HD // 2
    inverse_freq = jnp.float32(ROPE_BASE) ** (-(jnp.arange(half_dim, dtype=jnp.float32) * (2.0 / HD)))
    angles = (jnp.arange(count) % MAXLEN).astype(jnp.float32)[:, None] * inverse_freq[None, :]
    return (jnp.cos(angles)[:, None, :], jnp.sin(angles)[:, None, :])

def rotate(values, cos_table, sin_table):
    half_dim = values.shape[-1] // 2
    front = values[..., :half_dim]
    behind = values[..., half_dim:]
    return jnp.concatenate([front * cos_table - behind * sin_table, behind * cos_table + front * sin_table], axis=-1)

def attend_one(packed):
    queries, key_rows, value_rows, length = packed
    key_live = jnp.arange(MAXLEN) < length
    scores = low_back(jnp.einsum('qhe,khe->hqk', queries, key_rows, precision=HIGH) * HD ** (-0.5))
    pair_live = key_live[None, :, None] & key_live[None, None, :]
    top_logit = lax.optimization_barrier(jnp.max(jnp.where(pair_live, scores, NEG_FILL), axis=(1, 2)))
    masked = jnp.where(key_live[None, None, :], scores, NEG_FILL)
    row_peak = lax.optimization_barrier(jnp.max(masked, axis=-1, keepdims=True))
    weights = jnp.exp(masked - row_peak)
    probs = weights / lax.optimization_barrier(jnp.sum(weights, axis=-1, keepdims=True))
    attended = jnp.einsum('hqk,khe->qhe', low(probs), value_rows, precision=HIGH)
    return (jnp.where(key_live[:, None, None], attended, 0.0), top_logit)

def group_forward(inputs_val, lengths_grp, qkv_weight, out_weight, gain_a, bias_a, gate_up_weight, down_weight, gain_f, bias_f):
    count = inputs_val.shape[0]
    group_d = D // N_TENSOR
    group_f = FF // N_TENSOR
    projected = jnp.concatenate([matmul(low_back(inputs_val), qkv_weight[:, :, g * group_d:(g + 1) * group_d]) for g in range(N_TENSOR)], axis=2)
    projected = low_back(projected).reshape(count, 3, H, HD)
    cos_table, sin_table = rotary_tables(count)
    seq_shape = (SEQ_GRP, MAXLEN, H, HD)
    queries = low(rotate(projected[:, 0], cos_table, sin_table)).reshape(seq_shape)
    key_rows = low(rotate(projected[:, 1], cos_table, sin_table)).reshape(seq_shape)
    value_rows = low(projected[:, 2]).reshape(seq_shape)
    attended, top_logit = lax.map(jax.checkpoint(attend_one), (queries, key_rows, value_rows, lengths_grp))
    attended_low = low(low_back(attended.reshape(count, D)))
    partials_attn = [low(matmul(attended_low[:, g * group_d:(g + 1) * group_d], out_weight[g * group_d:(g + 1) * group_d])) for g in range(N_TENSOR)]
    branch_attn = low_back(sum(partials_attn))
    normed = layer_norm(inputs_val + branch_attn, gain_a, bias_a)
    normed_low = low(normed)
    gate_up = jnp.concatenate([matmul(low_back(normed_low), gate_up_weight[:, :, g * group_f:(g + 1) * group_f]) for g in range(N_TENSOR)], axis=2)
    gate_up = low_back(gate_up)
    hidden = low(jax.nn.silu(gate_up[:, 0]) * gate_up[:, 1])
    partials_ffn = [low(matmul(hidden[:, g * group_f:(g + 1) * group_f], down_weight[g * group_f:(g + 1) * group_f])) for g in range(N_TENSOR)]
    branch_ffn = low_back(sum(partials_ffn))
    return (layer_norm(normed + branch_ffn, gain_f, bias_f), lax.optimization_barrier(jnp.max(top_logit, axis=0)))

def reference(layer_input, output_grad, source_row, dest_row, seq_lengths, w_qkv, w_out, gain_attn, bias_attn, w_gate_up, w_down, gain_ffn, bias_ffn):
    group_rows = SEQ_GRP * MAXLEN
    inputs_work = layer_input.astype(jnp.float32)[source_row].reshape(N_DP, group_rows, D)
    grads_work = output_grad.astype(jnp.float32)[source_row].reshape(N_DP, group_rows, D)
    lengths_all = seq_lengths.reshape(N_DP, SEQ_GRP)
    weights = tuple((weight_arr.astype(jnp.float32) for weight_arr in (w_qkv, w_out, gain_attn, bias_attn, w_gate_up, w_down, gain_ffn, bias_ffn)))

    def step_group(running, packed):
        inputs_grp, grads_grp, lengths_grp = packed

        def forward(inputs_val, *weight_vals):
            return group_forward(inputs_val, lengths_grp, *weight_vals)
        result, pull_back, top_logit = jax.vjp(forward, inputs_grp, *weights, has_aux=True)
        pulled = pull_back(grads_grp)
        updated = tuple((total + piece for total, piece in zip(running, pulled[1:])))
        return (updated, (result, pulled[0], top_logit))
    zeros_init = tuple((jnp.zeros_like(weight_arr) for weight_arr in weights))
    summed, (outputs, input_grads, top_logits) = lax.scan(step_group, zeros_init, (inputs_work, grads_work, lengths_all))
    layer_output = outputs.reshape(TOKENS, D)[dest_row].astype(jnp.bfloat16)
    input_grad = input_grads.reshape(TOKENS, D)[dest_row].astype(jnp.bfloat16)
    head_top = lax.optimization_barrier(jnp.max(top_logits, axis=0))
    factor = jnp.sqrt(CLIP_AT / jnp.maximum(head_top, CLIP_AT))
    column = jnp.repeat(factor, HD)
    scaling = jnp.stack([column, column, jnp.ones_like(column)])
    clipped = weights[0] * scaling[None, :, :]
    return (layer_output, input_grad, summed[0], summed[1], summed[2], summed[3], summed[4], summed[5], summed[6], summed[7], clipped)
```

```python
import functools

import jax
import jax.numpy as jnp
import numpy as np
from jax import lax
from jax.experimental import pallas as pl
from jax.experimental.pallas import tpu as pltpu
from jax.sharding import PartitionSpec as P

H = 12
HD = 64
ROPE_BASE = 1000
MAXLEN = 1024
CLIP_AT = 4
NEG_FILL = -1e30
NORM_EPS = 1e-12

BF = jnp.bfloat16
F32 = jnp.float32
QB = 256
NB = MAXLEN // QB
ROWS = 3 * QB
WINDOWS = np.array(
    [
        [0, 1, 2, 3, 0, 1, 2, 3, 0, 1, 2, 3],
        [3, 4, 5, 0, 1, 2, 6, 7, 1, 2, 6, 7],
        [6, 7, 0, 1, 6, 7, 0, 1, 2, 3, 4, 5],
        [5, 0, 1, 2, 5, 0, 1, 2, 5, 0, 1, 2],
    ],
    np.int32,
)
VMEM = pltpu.VMEM
SMEM_SPEC = pl.BlockSpec(memory_space=pltpu.SMEM)
ANY_SPEC = pl.BlockSpec(memory_space=pl.ANY)
LIMIT = 60 * 1024 * 1024


def params():
    return pltpu.CompilerParams(vmem_limit_bytes=LIMIT)


def cost(flops, nbytes):
    return pl.CostEstimate(flops=int(flops), bytes_accessed=int(nbytes), transcendentals=0)


def nn(a, b):
    return lax.dot_general(a, b, (((1,), (0,)), ((), ())), preferred_element_type=F32)


def nt(a, b):
    return lax.dot_general(a, b, (((1,), (1,)), ((), ())), preferred_element_type=F32)


def tn(a, b):
    return lax.dot_general(a, b, (((0,), (0,)), ((), ())), preferred_element_type=F32)


def one_hot(index, rows, columns, along):
    at = lax.broadcasted_iota(jnp.int32, (rows, columns), along)
    return jnp.where(at == index, 1.0, 0.0).astype(BF)


def full(shape):
    return pl.BlockSpec(shape, lambda *_: (0,) * len(shape))


def order_rows(index, rows, along):
    def body(i_ref, x_ref, o_ref):
        pick = one_hot(i_ref[...], ROWS, ROWS, along)
        o_ref[...] = nn(pick, x_ref[...]).astype(BF)

    n, d = rows.shape
    return pl.pallas_call(
        body,
        out_shape=jax.ShapeDtypeStruct((n, d), BF),
        compiler_params=params(),
        cost_estimate=cost(2 * n * n * d, 4 * n * d),
        name="order_rows",
    )(index, rows)


def piece_copies(pieces, where, sems, spot):
    z, x = spot
    across, column_pieces = where
    out = []
    zp, xp = column_pieces
    for k in range(4):
        for r in range(2):
            if r == 0:
                src = zp.at[k]
            elif isinstance(xp, tuple):
                src = xp[k // 2].at[k % 2]
            else:
                src = xp.at[k]
            dst = across.at[lax.rem(z + 4 - k, 4), jnp.bitwise_xor(x, r)]
            out.append(pltpu.make_async_copy(src, dst, sems.at[2 * k + r]))
    return out


def slot_sources(pieces, slot):
    c, y = slot // 2, slot % 2
    zp, xp, yp, da, db = pieces[5 * c : 5 * c + 5]
    return (zp, xp) if y == 0 else (yp, (da, db))


def load_all(pieces, buffer, sems, cfg):
    copies = []
    for slot in range(4):
        copies += piece_copies(
            pieces, (buffer.at[slot], slot_sources(pieces, slot)), sems.at[slot], (cfg[0], cfg[1])
        )
    for c in copies:
        c.start()
    return copies


def half_turn(u, lane):
    return jnp.where(lane, pltpu.roll(u, 96, 1), pltpu.roll(u, 32, 1))


def qkv_kernel(cfg, recv, place, cos, sin, *rest):
    pieces = rest[:10]
    xw_ref, q_ref, kv_ref, buffer, qk, sems = rest[10:]
    copies = load_all(pieces, buffer, sems, cfg)
    pick = one_hot(place[...], ROWS, ROWS, 1)
    xw = nn(pick, recv[...]).astype(BF)
    xw_ref[...] = xw
    for c in copies:
        c.wait()
    d = xw.shape[1]
    for t in range(4):
        w = buffer[cfg[2 + t]].reshape(d, d)
        res = nn(xw, w[:, : d * 3 // 4])
        g = d // 4
        qk[:, g * t : g * t + g] = res[:, :g]
        qk[:, d + g * t : d + g * t + g] = res[:, g : 2 * g]
        kv_ref[:, d + g * t : d + g * t + g] = res[:, 2 * g :].astype(BF)
    lane = lax.broadcasted_iota(jnp.int32, (ROWS, 128), 1) % HD < HD // 2
    for s in range(2 * d // 128):
        u = qk[:, 128 * s : 128 * s + 128]
        r = (u * cos[...] + half_turn(u, lane) * sin[...]).astype(BF)
        if s < d // 128:
            q_ref[:, 128 * s : 128 * s + 128] = r
        else:
            kv_ref[:, 128 * s - d : 128 * s - d + 128] = r


def project(cfg, recv, place, cos, sin, pieces):
    n, d = recv.shape
    return pl.pallas_call(
        qkv_kernel,
        out_shape=(
            jax.ShapeDtypeStruct((n, d), BF),
            jax.ShapeDtypeStruct((n, d), BF),
            jax.ShapeDtypeStruct((n, 2 * d), BF),
        ),
        in_specs=[SMEM_SPEC] + [pl.BlockSpec(memory_space=VMEM)] * 4 + [ANY_SPEC] * 10,
        out_specs=[pl.BlockSpec(memory_space=VMEM)] * 3,
        scratch_shapes=[
            VMEM((4, 4, 2, 96, d), BF),
            VMEM((n, 2 * d), F32),
            pltpu.SemaphoreType.DMA((4, 8)),
        ],
        compiler_params=params(),
        cost_estimate=cost(2 * n * d * 4 * d, 12 * d * d),
        name="project",
    )(cfg, recv, place, cos, sin, *pieces)


def fill_windows(dst, own, mate, over):
    dst[0:3] = own[...].reshape(3, QB, 128)
    dst[3:6] = mate[...].reshape(3, QB, 128)
    dst[6:8] = over[...].reshape(2, QB, 128)


def window(blocks, att, b):
    return jnp.concatenate([blocks[att[NB * b + j]] for j in range(NB)], axis=0)


def attend_kernel(att, q, ko, vo, km, vm, kx, vx, out, probs, top, kb, vb):
    fill_windows(kb, ko, km, kx)
    fill_windows(vb, vo, vm, vx)
    low_half = lax.broadcasted_iota(jnp.int32, (QB, 128), 1) < HD
    key_at = lax.broadcasted_iota(jnp.int32, (QB, MAXLEN), 1)
    row_at = lax.broadcasted_iota(jnp.int32, (QB, 1), 0)
    tops = [jnp.full((1, 1), NEG_FILL, F32)] * 2
    for b in range(3):
        length = att[12 + b]
        kw, vw = window(kb, att, b), window(vb, att, b)
        live = row_at + att[15 + b] < length
        qq = q[QB * b : QB * b + QB]
        heads = []
        for h in range(2):
            mine = low_half if h == 0 else jnp.logical_not(low_half)
            scores = nt(jnp.where(mine, qq, jnp.zeros_like(qq)), kw) * HD**-0.5
            scores = jnp.where(key_at < length, scores, NEG_FILL)
            peak = jnp.max(scores, axis=1, keepdims=True)
            weights = jnp.exp(scores - peak)
            inverse = 1.0 / jnp.sum(weights, axis=1, keepdims=True)
            low = (weights * inverse).astype(BF)
            probs[h, b] = low
            heads.append(nn(low, vw))
            best = jnp.max(jnp.where(live, peak, NEG_FILL), axis=0, keepdims=True)
            tops[h] = jnp.maximum(tops[h], best)
        mixed = jnp.where(low_half, heads[0], heads[1])
        out[QB * b : QB * b + QB] = jnp.where(live, mixed, 0.0).astype(BF)
    for h in range(2):
        top[0, h] = jnp.broadcast_to(tops[h][0], (128,))


def kv_specs(rows, pairs):
    return [
        pl.BlockSpec((rows, 128), lambda i: (0, i)),
        pl.BlockSpec((rows, 128), lambda i: (0, pairs + i)),
    ]


def attend(att, q, own, mate, over):
    n, d = q.shape
    pairs = d // 128
    return pl.pallas_call(
        attend_kernel,
        grid=(pairs,),
        out_shape=(
            jax.ShapeDtypeStruct((n, d), BF),
            jax.ShapeDtypeStruct((2 * pairs, 3, QB, MAXLEN), BF),
            jax.ShapeDtypeStruct((pairs, 2, 128), F32),
        ),
        in_specs=[SMEM_SPEC, pl.BlockSpec((n, 128), lambda i: (0, i))]
        + kv_specs(n, pairs)
        + kv_specs(n, pairs)
        + kv_specs(2 * QB, pairs),
        out_specs=(
            pl.BlockSpec((n, 128), lambda i: (0, i)),
            pl.BlockSpec((2, 3, QB, MAXLEN), lambda i: (i, 0, 0, 0)),
            pl.BlockSpec((1, 2, 128), lambda i: (i, 0, 0)),
        ),
        scratch_shapes=[VMEM((8, QB, 128), BF)] * 2,
        compiler_params=params(),
        cost_estimate=cost(16 * n * MAXLEN * d, 26 * n * d),
        name="attend",
    )(att, q, own, own, mate, mate, over, over)


def mean(v):
    return jnp.mean(v, axis=-1, keepdims=True)


def norm(values):
    centred = values - mean(values)
    inverse = lax.rsqrt(mean(centred * centred) + NORM_EPS)
    return centred * inverse, inverse


def norm_back(upstream, unit, inverse, gain):
    scaled = upstream * gain
    return inverse * (scaled - mean(scaled) - unit * mean(scaled * unit))


def out_kernel(cfg, att, xw, gains, *rest):
    pieces = rest[:10]
    low_ref, unit_ref, inv_ref, buffer, sems = rest[10:]
    copies = load_all(pieces, buffer, sems, cfg)
    for c in copies:
        c.wait()
    d = xw.shape[1]
    g = d // 4
    z1 = xw[...].astype(F32)
    for t in range(4):
        w = buffer[cfg[2 + t]].reshape(d, d)
        z1 = z1 + nt(att[:, g * t : g * t + g], w[:, 3 * g :])
    unit, inverse = norm(z1)
    unit_ref[...] = unit
    inv_ref[...] = jnp.broadcast_to(inverse, inv_ref.shape)
    low_ref[...] = (unit * gains[0:1] + gains[1:2]).astype(BF)


def out_norm(cfg, att, xw, gains, pieces):
    n, d = xw.shape
    return pl.pallas_call(
        out_kernel,
        out_shape=(
            jax.ShapeDtypeStruct((n, d), BF),
            jax.ShapeDtypeStruct((n, d), F32),
            jax.ShapeDtypeStruct((n, 128), F32),
        ),
        in_specs=[SMEM_SPEC] + [pl.BlockSpec(memory_space=VMEM)] * 3 + [ANY_SPEC] * 10,
        out_specs=[pl.BlockSpec(memory_space=VMEM)] * 3,
        scratch_shapes=[VMEM((4, 4, 2, 96, d), BF), pltpu.SemaphoreType.DMA((4, 8))],
        compiler_params=params(),
        cost_estimate=cost(2 * n * d * d, 20 * d * d),
        name="out_norm",
    )(cfg, att, xw, gains, *pieces)


def stream(pieces, buffer, sems, cfg):
    s = pl.program_id(0)

    def start(slot):
        for c in piece_copies(
            pieces,
            (buffer.at[slot % 2], slot_sources(pieces, slot)),
            sems.at[slot % 2],
            (cfg[0], cfg[1]),
        ):
            c.start()

    @pl.when(s == 0)
    def _():
        start(0)

    for slot in range(1, 4):

        @pl.when(s == slot - 1)
        def _(slot=slot):
            start(slot)

    at = lax.rem(s, 2)
    for i in range(8):
        pltpu.make_async_copy(pieces[0].at[0], buffer.at[at, i // 2, i % 2], sems.at[at, i]).wait()
    n = 8 * buffer.shape[3]
    return buffer[at].reshape(n, buffer.shape[4])


def ffn_kernel(cfg, low, unit1, gains, place_col, place_row, recv, *rest):
    pieces = rest[:10]
    gu_ref, sent_ref, gz2_ref, sums_ref, buffer, acc, sems = rest[10:]
    d = low.shape[1]
    s = pl.program_id(0)
    w = stream(pieces, buffer, sems, cfg)
    gate = nn(low[...], w[:, :d])
    up = nn(low[...], w[:, d : 2 * d])
    gu_ref[0, :, :d] = gate.astype(BF)
    gu_ref[0, :, d:] = up.astype(BF)
    hidden = (gate * jax.nn.sigmoid(gate) * up).astype(BF)
    part = nt(hidden, w[:, 2 * d :])

    @pl.when(s == 0)
    def _():
        acc[...] = part

    @pl.when(s > 0)
    def _():
        acc[...] += part

    @pl.when(s == 3)
    def _():
        z2 = unit1[...] * gains[0:1] + gains[1:2] + acc[...]
        unit, inverse = norm(z2)
        y = (unit * gains[2:3] + gains[3:4]).astype(BF)
        sent_ref[...] = nn(one_hot(place_row[...], ROWS, ROWS, 0), y).astype(BF)
        up_grad = nn(one_hot(place_col[...], ROWS, ROWS, 1), recv[...])
        gz2_ref[...] = norm_back(up_grad, unit, inverse, gains[2:3])
        sums_ref[0:1] = jnp.sum(up_grad * unit, axis=0, keepdims=True)
        sums_ref[1:2] = jnp.sum(up_grad, axis=0, keepdims=True)


def feed_forward(cfg, low, unit1, gains, place_col, place_row, recv, pieces):
    n, d = low.shape
    return pl.pallas_call(
        ffn_kernel,
        grid=(4,),
        out_shape=(
            jax.ShapeDtypeStruct((4, n, 2 * d), BF),
            jax.ShapeDtypeStruct((n, d), BF),
            jax.ShapeDtypeStruct((n, d), F32),
            jax.ShapeDtypeStruct((2, d), F32),
        ),
        in_specs=[SMEM_SPEC] + [pl.BlockSpec(memory_space=VMEM)] * 6 + [ANY_SPEC] * 10,
        out_specs=(
            pl.BlockSpec((1, n, 2 * d), lambda s: (s, 0, 0)),
            full((n, d)),
            full((n, d)),
            full((2, d)),
        ),
        scratch_shapes=[
            VMEM((2, 4, 2, 96, 3 * d), BF),
            VMEM((n, d), F32),
            pltpu.SemaphoreType.DMA((2, 8)),
        ],
        compiler_params=params(),
        cost_estimate=cost(24 * n * d * d, 50 * d * d),
        name="feed_forward",
    )(cfg, low, unit1, gains, place_col, place_row, recv, *pieces)


def ffn_back_kernel(cfg, gz2, gu, unit1, inv1, gains, *rest):
    pieces = rest[:10]
    g_ref, dgu_ref, hid_ref, gz1_ref, gz1_low_ref, sums_ref, buffer, acc, sems = rest[10:]
    d = gz2.shape[1]
    s = pl.program_id(0)
    w = stream(pieces, buffer, sems, cfg)

    @pl.when(s == 0)
    def _():
        g_ref[...] = gz2[...].astype(BF)
        acc[...] = gz2[...]

    grad_hidden = nn(g_ref[...], w[:, 2 * d :])
    gate = gu[0, :, :d].astype(F32)
    up = gu[0, :, d:].astype(F32)
    sig = jax.nn.sigmoid(gate)
    silu = gate * sig
    hid_ref[0] = (silu * up).astype(BF)
    dgate = (grad_hidden * up * sig * (1.0 + gate * (1.0 - sig))).astype(BF)
    dup = (grad_hidden * silu).astype(BF)
    dgu_ref[0, :, :d] = dgate
    dgu_ref[0, :, d:] = dup
    acc[...] += nt(dgate, w[:, :d]) + nt(dup, w[:, d : 2 * d])

    @pl.when(s == 3)
    def _():
        grad = acc[...]
        unit = unit1[...]
        back = norm_back(grad, unit, inv1[:, 0:1], gains[0:1])
        gz1_ref[...] = back
        gz1_low_ref[...] = back.astype(BF)
        sums_ref[0:1] = jnp.sum(grad * unit, axis=0, keepdims=True)
        sums_ref[1:2] = jnp.sum(grad, axis=0, keepdims=True)


def ffn_back(cfg, gz2, gu, unit1, inv1, gains, pieces):
    n, d = gz2.shape
    return pl.pallas_call(
        ffn_back_kernel,
        grid=(4,),
        out_shape=(
            jax.ShapeDtypeStruct((n, d), BF),
            jax.ShapeDtypeStruct((4, n, 2 * d), BF),
            jax.ShapeDtypeStruct((4, n, d), BF),
            jax.ShapeDtypeStruct((n, d), F32),
            jax.ShapeDtypeStruct((n, d), BF),
            jax.ShapeDtypeStruct((2, d), F32),
        ),
        in_specs=[
            SMEM_SPEC,
            pl.BlockSpec(memory_space=VMEM),
            pl.BlockSpec((1, n, 2 * d), lambda s: (s, 0, 0)),
        ]
        + [pl.BlockSpec(memory_space=VMEM)] * 3
        + [ANY_SPEC] * 10,
        out_specs=(
            full((n, d)),
            pl.BlockSpec((1, n, 2 * d), lambda s: (s, 0, 0)),
            pl.BlockSpec((1, n, d), lambda s: (s, 0, 0)),
            full((n, d)),
            full((n, d)),
            full((2, d)),
        ),
        scratch_shapes=[
            VMEM((2, 4, 2, 96, 3 * d), BF),
            VMEM((n, d), F32),
            pltpu.SemaphoreType.DMA((2, 8)),
        ],
        compiler_params=params(),
        cost_estimate=cost(24 * n * d * d, 80 * d * d),
        name="ffn_back",
    )(cfg, gz2, gu, unit1, inv1, gains, *pieces)


def put_blocks(out, grad, cfg, columns):
    for b in range(8):
        zr = lax.rem(b // 2 + 4 - cfg[0], 4)
        out[0, jnp.bitwise_xor(cfg[1], b % 2), zr, :, columns] = grad[96 * b : 96 * b + 96].astype(
            BF
        )


def ffn_grad_kernel(cfg, low, g, dgu, hid, out):
    d = low.shape[1]
    put_blocks(out, tn(low[...], dgu[0, :, :d]), cfg, pl.ds(0, d))
    put_blocks(out, tn(low[...], dgu[0, :, d:]), cfg, pl.ds(d, d))
    put_blocks(out, tn(g[...], hid[0]), cfg, pl.ds(2 * d, d))


def ffn_grads(cfg, low, g, dgu, hid, which):
    n, d = low.shape
    return pl.pallas_call(
        ffn_grad_kernel,
        grid=(2,),
        out_shape=jax.ShapeDtypeStruct((2, 2, 4, 96, 3 * d), BF),
        in_specs=[
            SMEM_SPEC,
            full((n, d)),
            full((n, d)),
            pl.BlockSpec((1, n, 2 * d), lambda s: (2 * which + s, 0, 0)),
            pl.BlockSpec((1, n, d), lambda s: (2 * which + s, 0, 0)),
        ],
        out_specs=pl.BlockSpec((1, 2, 4, 96, 3 * d), lambda s: (s, 0, 0, 0, 0)),
        compiler_params=params(),
        cost_estimate=cost(12 * n * d * d, 20 * d * d),
        name="ffn_grads",
    )(cfg, low, g, dgu, hid)


def att_grad_kernel(cfg, att, gz1_low, live, *rest):
    pieces = rest[:10]
    ga_ref, buffer, sems = rest[10:]
    copies = load_all(pieces, buffer, sems, cfg)
    for c in copies:
        c.wait()
    d = att.shape[1]
    g = d // 4
    for t in range(4):
        w = buffer[cfg[2 + t]].reshape(d, d)
        part = nn(gz1_low[...], w[:, 3 * g :])
        ga_ref[:, g * t : g * t + g] = jnp.where(live[...] > 0, part, 0.0).astype(BF)


def att_grad(cfg, att, gz1_low, live, pieces):
    n, d = att.shape
    return pl.pallas_call(
        att_grad_kernel,
        out_shape=jax.ShapeDtypeStruct((n, d), BF),
        in_specs=[SMEM_SPEC] + [pl.BlockSpec(memory_space=VMEM)] * 3 + [ANY_SPEC] * 10,
        out_specs=pl.BlockSpec(memory_space=VMEM),
        scratch_shapes=[VMEM((4, 4, 2, 96, d), BF), pltpu.SemaphoreType.DMA((4, 8))],
        compiler_params=params(),
        cost_estimate=cost(2 * n * d * d, 12 * d * d),
        name="att_grad",
    )(cfg, att, gz1_low, live, *pieces)


def attend_back_kernel(
    att, q, ga, out, cos, sin, probs, ko, vo, km, vm, kx, vx,
    dq_ref, dko, dvo, dkm, dvm, dkx, dvx, kb, vb, dk, dv,
):
    fill_windows(kb, ko, km, kx)
    fill_windows(vb, vo, vm, vx)
    dk[...] = jnp.zeros_like(dk)
    dv[...] = jnp.zeros_like(dv)
    low_half = lax.broadcasted_iota(jnp.int32, (QB, 128), 1) < HD
    turn = lax.broadcasted_iota(jnp.int32, (QB, 128), 1) % HD < HD // 2
    zero = jnp.zeros((QB, 128), BF)
    for b in range(3):
        kw, vw = window(kb, att, b), window(vb, att, b)
        rows = slice(QB * b, QB * b + QB)
        qq, gg, oo = q[rows], ga[rows], out[rows]
        dot = gg.astype(F32) * oo.astype(F32)
        dks = dvs = dqs = None
        for h in range(2):
            mine = low_half if h == 0 else jnp.logical_not(low_half)
            gh = jnp.where(mine, gg, zero)
            qh = jnp.where(mine, qq, zero)
            inner = jnp.sum(jnp.where(mine, dot, 0.0), axis=1, keepdims=True)
            p = probs[h, b]
            ds = (p.astype(F32) * (nt(gh, vw) - inner)).astype(BF)
            dqh = nn(ds, kw)
            dkh, dvh = tn(ds, qh), tn(p, gh)
            dks = dkh if dks is None else dks + dkh
            dvs = dvh if dvs is None else dvs + dvh
            dqs = dqh if dqs is None else jnp.where(low_half, dqs, dqh)
        for j in range(NB):
            at = att[NB * b + j]
            dk[at] += dks[QB * j : QB * j + QB]
            dv[at] += dvs[QB * j : QB * j + QB]
        dqs = dqs * HD**-0.5
        dq_ref[rows] = (dqs * cos[rows] - half_turn(dqs, turn) * sin[rows]).astype(BF)
    for at, (dk_ref, dv_ref, count) in ((0, (dko, dvo, 3)), (3, (dkm, dvm, 3)), (6, (dkx, dvx, 2))):
        dk_ref[...] = (dk[at : at + count].reshape(count * QB, 128) * HD**-0.5).astype(dk_ref.dtype)
        dv_ref[...] = dv[at : at + count].reshape(count * QB, 128).astype(dv_ref.dtype)


def attend_back(att, q, ga, out, cos, sin, probs, own, mate, over):
    n, d = q.shape
    pairs = d // 128
    slab = pl.BlockSpec((n, 128), lambda i: (0, i))
    slab_x = pl.BlockSpec((2 * QB, 128), lambda i: (0, i))
    shape = jax.ShapeDtypeStruct
    return pl.pallas_call(
        attend_back_kernel,
        grid=(pairs,),
        out_shape=(
            shape((n, d), BF),
            shape((n, d), F32),
            shape((n, d), F32),
            shape((n, d), BF),
            shape((n, d), BF),
            shape((2 * QB, d), BF),
            shape((2 * QB, d), BF),
        ),
        in_specs=[SMEM_SPEC, slab, slab, slab, full((n, 128)), full((n, 128))]
        + [pl.BlockSpec((2, 3, QB, MAXLEN), lambda i: (i, 0, 0, 0))]
        + kv_specs(n, pairs)
        + kv_specs(n, pairs)
        + kv_specs(2 * QB, pairs),
        out_specs=(slab, slab, slab, slab, slab, slab_x, slab_x),
        scratch_shapes=[VMEM((8, QB, 128), BF)] * 2 + [VMEM((8, QB, 128), F32)] * 2,
        compiler_params=params(),
        cost_estimate=cost(32 * n * MAXLEN * d, 50 * n * d),
        name="attend_back",
    )(att, q, ga, out, cos, sin, probs, own, own, mate, mate, over, over)


def last_kernel(cfg, xw, att, gz1, gz1_low, dq, dko, dvo, dkm, dvm, dkx, dvx, cos, sin, place, *rest):
    pieces = rest[:10]
    sent_ref, grads, dk, dv, buffer, sems = rest[10:]
    copies = load_all(pieces, buffer, sems, cfg)
    d = xw.shape[1]
    g = d // 4
    dkf = dko[...] + dkm[...].astype(F32)
    dko[...] = dkf
    dvo[...] = dvo[...] + dvm[...].astype(F32)
    at = pl.multiple_of(cfg[6], QB)
    dko[pl.ds(at, 2 * QB)] += dkx[...].astype(F32)
    dvo[pl.ds(at, 2 * QB)] += dvx[...].astype(F32)
    lane = lax.broadcasted_iota(jnp.int32, (ROWS, 128), 1) % HD < HD // 2
    for s in range(d // 128):
        u = dko[:, 128 * s : 128 * s + 128]
        dk[:, 128 * s : 128 * s + 128] = (u * cos[...] - half_turn(u, lane) * sin[...]).astype(BF)
    dv[...] = dvo[...].astype(BF)
    for c in copies:
        c.wait()
    gx = gz1[...]
    for t in range(4):
        slot = cfg[2 + t]
        columns = slice(g * t, g * t + g)
        both = jnp.concatenate([dq[:, columns], dk[:, columns], dv[:, columns]], axis=1)
        w = buffer[slot].reshape(d, d)
        gx = gx + nt(both, w[:, : 3 * g])
        whole = jnp.concatenate(
            [tn(xw[...], both), tn(gz1_low[...], att[:, columns])], axis=1
        )
        for b in range(8):
            zr = lax.rem(b // 2 + 4 - cfg[0], 4)
            grads[slot, jnp.bitwise_xor(cfg[1], b % 2), zr] = whole[96 * b : 96 * b + 96].astype(BF)
    sent_ref[...] = nn(one_hot(place[...], ROWS, ROWS, 0), gx.astype(BF)).astype(BF)


def last(cfg, xw, att, gz1, gz1_low, dq, parts, cos, sin, place, pieces):
    n, d = xw.shape
    return pl.pallas_call(
        last_kernel,
        out_shape=(
            jax.ShapeDtypeStruct((n, d), BF),
            jax.ShapeDtypeStruct((4, 2, 4, 96, d), BF),
        ),
        in_specs=[SMEM_SPEC] + [pl.BlockSpec(memory_space=VMEM)] * 14 + [ANY_SPEC] * 10,
        out_specs=[pl.BlockSpec(memory_space=VMEM)] * 2,
        scratch_shapes=[
            VMEM((n, d), BF),
            VMEM((n, d), BF),
            VMEM((4, 4, 2, 96, d), BF),
            pltpu.SemaphoreType.DMA((4, 8)),
        ],
        compiler_params=params(),
        cost_estimate=cost(16 * n * d * d, 60 * d * d),
        name="last",
    )(cfg, xw, att, gz1, gz1_low, dq, *parts, cos, sin, place, *pieces)


def chip_plan(dp_count, tensor_count):
    return dp_count == 8 and tensor_count == 4


def swap_x(a):
    return lax.ppermute(a, "dp", [(i, i ^ 1) for i in range(lax.axis_size("dp"))])


def swap_y(a):
    return lax.ppermute(a, "tensor", [(i, i ^ 2) for i in range(4)])


def swap_core(a):
    return lax.ppermute(a, "tensor", [(i, i ^ 1) for i in range(4)])


def step_z(a, k):
    n = lax.axis_size("dp")
    return lax.ppermute(a, "dp", [(i, (i + 2 * k) % n) for i in range(n)])


def gather_pieces(shard, direct):
    if direct:
        zp = jnp.stack([shard] + [step_z(shard, k) for k in (1, 2, 3)])
        xp, yp = swap_x(zp), swap_y(zp)
        da, db = swap_y(xp[0:2]), swap_x(yp[2:4])
        mine = (zp, xp, yp, da, db)
        return mine + tuple(swap_core(a) for a in mine)
    whole = lax.all_gather(shard, "dp", axis=0, tiled=True)
    whole = lax.all_gather(whole, "tensor", axis=0)
    c = shard.shape[1]
    whole = whole.reshape(2, 2, 4, 2, 96, c)[:, :, np.array([0, 3, 2, 1])]
    out = []
    for core in range(2):
        w0, w1 = whole[0, core], whole[1, core]
        out += [w0[:, 0], w0[:, 1], w1[:, 0], w1[0:2, 1], w1[2:4, 1]]
    return tuple(out)


def add_low(*terms):
    total = terms[0].astype(F32)
    for t in terms[1:]:
        total = total + t.astype(F32)
    return total


def scatter_sums(far, near, direct):
    if direct:
        got = swap_core(far)
        half = add_low(near, got).astype(BF)
        ra, rb = swap_y(half[1, 1, 0:2]), swap_x(half[1, 1, 2:4])
        to_x = jnp.concatenate([add_low(half[0, 1, 0:2], ra).astype(BF), half[0, 1, 2:4]])
        to_y = jnp.concatenate([half[1, 0, 0:2], add_low(half[1, 0, 2:4], rb).astype(BF)])
        mine = add_low(half[0, 0], swap_x(to_x), swap_y(to_y)).astype(BF)
        return add_low(mine[0], *[step_z(mine[k], k) for k in (1, 2, 3)])
    both = jnp.stack([near, far])
    c = both.shape[-1]
    both = jnp.transpose(both, (1, 0, 3, 2, 4, 5)).reshape(4, 768, c)
    part = lax.psum_scatter(both, "tensor", scatter_dimension=0, tiled=True)[0]
    return lax.psum_scatter(part, "dp", scatter_dimension=0, tiled=True).astype(F32)


def to_all(a, axis):
    n = lax.axis_size(axis)
    return lax.all_to_all(
        jnp.broadcast_to(a[None], (n,) + a.shape), axis, split_axis=0, concat_axis=0, tiled=True
    )


def exchange(rows):
    return lax.all_to_all(rows, "dp", split_axis=0, concat_axis=0, tiled=True)


def ranks(key):
    return jnp.sum((key[None, :] < key[:, None]).astype(jnp.int32), axis=1)


def per_device(
    layer_input,
    output_grad,
    source_row,
    dest_row,
    seq_lengths,
    w_qkv,
    w_out,
    gain_attn,
    bias_attn,
    w_gate_up,
    w_down,
    gain_ffn,
    bias_ffn,
):
    n, d = layer_input.shape
    dp_count, tensor_count = lax.axis_size("dp"), lax.axis_size("tensor")
    direct = chip_plan(dp_count, tensor_count)
    group_rows = n * tensor_count
    dp, t = lax.axis_index("dp"), lax.axis_index("tensor")
    width = w_qkv.shape[0]
    rank = ranks(dest_row)
    place = ranks(source_row // group_rows * n + jnp.arange(n, dtype=jnp.int32))
    rank_row, rank_col = rank.reshape(1, n), rank.reshape(n, 1)
    place_row, place_col = place.reshape(1, n), place.reshape(n, 1)
    shard_a = jnp.concatenate([w_qkv.reshape(width, -1), w_out.T], axis=1)
    shard_f = jnp.concatenate([w_gate_up.reshape(width, -1), w_down.T], axis=1)
    if direct:
        z, x, y, c = dp // 2, dp % 2, t // 2, t % 2
    else:
        z = x = y = c = jnp.int32(0)
    tt = jnp.arange(4, dtype=jnp.int32)
    slots = ((tt % 2) ^ c) * 2 + ((tt // 2) ^ y)
    over_at = jnp.where(t == 1, QB, 0)
    cfg = jnp.concatenate([jnp.stack([z, x]), slots, over_at[None]]).astype(jnp.int32)
    block = 3 * t + jnp.arange(3, dtype=jnp.int32)
    att = jnp.concatenate(
        [jnp.asarray(WINDOWS)[t], seq_lengths[block // NB], block % NB * QB]
    ).astype(jnp.int32)
    position = (t * n + jnp.arange(n, dtype=jnp.int32)) % MAXLEN
    live = (position < seq_lengths[(t * n + jnp.arange(n)) // MAXLEN]).astype(jnp.int32)[:, None]
    inverse_freq = F32(ROPE_BASE) ** (-(jnp.arange(HD // 2, dtype=F32) * (2.0 / HD)))
    angles = position.astype(F32)[:, None] * inverse_freq[None, :]
    cos_half, sin_half = jnp.cos(angles), jnp.sin(angles)
    cos = jnp.concatenate([cos_half] * 4, axis=1)
    sin = jnp.concatenate([-sin_half, sin_half] * 2, axis=1)

    pieces_a = gather_pieces(shard_a, direct)
    recv_x = exchange(order_rows(rank_row, layer_input, 0))
    vectors = jnp.stack([gain_attn, bias_attn, gain_ffn, bias_ffn]).astype(F32)
    gains = jnp.transpose(to_all(vectors, "dp").reshape(dp_count, 4, width), (1, 0, 2)).reshape(4, d)
    recv_g = exchange(order_rows(rank_row, output_grad, 0))
    pieces_f = gather_pieces(shard_f, direct)

    xw, q, kv = project(cfg, recv_x, place_col, cos, sin, pieces_a)
    across = [(1, 2), (2, 1)]
    mate = swap_core(kv)
    over = lax.ppermute(lax.dynamic_slice_in_dim(kv, over_at, 2 * QB, 0), "tensor", across)
    attended, probs, tops = attend(att, q, kv, mate, over)
    low, unit1, inv1 = out_norm(cfg, attended, xw, gains, pieces_a)
    gu, sent_y, gz2, sums_f = feed_forward(
        cfg, low, unit1, gains, place_col, place_row, recv_g, pieces_f
    )
    back_y = exchange(sent_y)
    g_low, dgu, hid, gz1, gz1_low, sums_a = ffn_back(cfg, gz2, gu, unit1, inv1, gains, pieces_f)
    far_f = ffn_grads(cfg, low, g_low, dgu, hid, 1)
    near_f = ffn_grads(cfg, low, g_low, dgu, hid, 0)
    own_f = scatter_sums(far_f, near_f, direct)
    ga = att_grad(cfg, attended, gz1_low, live, pieces_a)
    dq, dko, dvo, dkm, dvm, dkx, dvx = attend_back(
        att, q, ga, attended, cos, sin, probs, kv, mate, over
    )
    parts = (dko, dvo, swap_core(dkm), swap_core(dvm)) + tuple(
        lax.ppermute(a, "tensor", across) for a in (dkx, dvx)
    )
    sent_x, grads_a = last(
        cfg, xw, attended, gz1, gz1_low, dq, parts, cos, sin, place_row, pieces_a
    )
    back_x = exchange(sent_x)
    own_a = scatter_sums(grads_a[2:4], grads_a[0:2], direct)

    sums = jnp.concatenate([sums_a, sums_f]).reshape(4, dp_count, width)
    top = jnp.broadcast_to(tops[:, :, 0].reshape(1, H), (dp_count, H))
    packed = jnp.concatenate([jnp.transpose(sums, (1, 0, 2)).reshape(dp_count, -1), top], axis=1)
    stage = lax.all_to_all(packed, "dp", split_axis=0, concat_axis=0, tiled=True)
    stage = jnp.concatenate([jnp.sum(stage[:, :-H], axis=0), jnp.max(stage[:, -H:], axis=0)])
    stage = to_all(stage, "tensor").reshape(tensor_count, -1)
    own_sums = jnp.sum(stage[:, :-H], axis=0).reshape(4, width)
    head_top = jnp.max(stage[:, -H:], axis=0)
    heads = w_qkv.shape[2] // HD
    own_top = lax.dynamic_slice_in_dim(head_top, t * heads, heads, 0)
    factor = jnp.sqrt(CLIP_AT / jnp.maximum(own_top, CLIP_AT))
    column = jnp.repeat(factor, HD)
    scaling = jnp.stack([column, column, jnp.ones_like(column)])
    clipped = w_qkv.astype(F32) * scaling[None, :, :]

    g = d // 4
    return (
        order_rows(rank_col, back_y, 1),
        order_rows(rank_col, back_x, 1),
        own_a[:, : 3 * g].reshape(width, 3, g),
        own_a[:, 3 * g :].T,
        own_sums[0],
        own_sums[1],
        own_f[:, : 2 * d].reshape(width, 2, d),
        own_f[:, 2 * d :].T,
        own_sums[2],
        own_sums[3],
        clipped,
    )


def solution(mesh):
    return jax.shard_map(
        per_device,
        mesh=mesh,
        in_specs=(
            P(("dp", "tensor"), None),
            P(("dp", "tensor"), None),
            P(("dp", "tensor")),
            P(("dp", "tensor")),
            P("dp"),
            P("dp", None, "tensor"),
            P("tensor", "dp"),
            P("dp"),
            P("dp"),
            P("dp", None, "tensor"),
            P("tensor", "dp"),
            P("dp"),
            P("dp"),
        ),
        out_specs=(
            P(("dp", "tensor"), None),
            P(("dp", "tensor"), None),
            P("dp", None, "tensor"),
            P("tensor", "dp"),
            P("dp"),
            P("dp"),
            P("dp", None, "tensor"),
            P("tensor", "dp"),
            P("dp"),
            P("dp"),
            P("dp", None, "tensor"),
        ),
        check_vma=False,
    )
```
